512 devices in a mesh: dp: 64 (over z_hi, y, x), blk: 8 (over z_lo, core).
Axes of the slice: x: 4, y: 8, z: 8 (z_hi: 2, z_lo: 4; z = z_hi * 4 + z_lo), core: 2. Of those that a mesh axis runs over, the one named last changes fastest.
Arguments:
- train_act: bfloat16 [2048, 4096], P(('dp', 'blk')), may hold values from -3 to 3
- train_grad: bfloat16 [2048, 8192], P(('dp', 'blk')), may hold values from -3 to 3
- query_act: bfloat16 [256, 4096], P('dp', 'blk'), may hold values from -3 to 3
- query_grad: bfloat16 [256, 8192], P('dp'), may hold values from -3 to 3
- act_basis: bfloat16 [4096, 512], P('blk'), may hold values from -0.25 to 0.25
- grad_basis: bfloat16 [512, 8192], P(None, 'dp'), may hold values from -0.25 to 0.25
- eigenvalues: float32 [4096, 8192], P('blk', 'dp'), may hold values from 0.05 to 5
- example_ids: int32 [2048], replicated, may hold values from 0 to 127, never falling along the last dimension, each value on 1 to 48 neighbouring positions
- query_ids: int32 [256], replicated, may hold values from 0 to 15, never falling along the last dimension, each value on 1 to 48 neighbouring positions
Outputs:
- influence: float32 [128, 16], P('dp')
The draws below stay inside these ranges and needn't reach their ends.
Inputs may be any that keep to these rules, and one draw needn't show every extreme that they name: `example_ids`: the tokens of one training example are contiguous and ids never fall; every example has a token. `query_ids`: the tokens of one query are contiguous and ids never fall; every query has a token.
All inputs are finite; a program needn't handle non-finite values.
Results may differ from the reference program's by a relative error of at most 0.0007.
The reference program's roundings to bfloat16 on the way (of `act_rot`, `query_rot`, `grad_rot`, `query_grad_rot` and `precond`) count: a program that leaves them out, or rounds other values in their place, can miss the bound.
Values may be sent and summed in bfloat16 or wider, within the bound.
No kernel may reach another device: no remote copies, remote signals or barrier semaphores. Data moves between devices by JAX's collectives and lax.ppermute only.
A program may use at most 64 MiB of HBM per device.

```python
import math
import jax
import jax.numpy as jnp
import numpy as np
from jax import lax

D = 4096
FF = 8192
BLOCK = 512
TOK_DEV = 4
QUERIES = 16
EX_DP = 2
TOKENS = 2048
QTOKENS = 256
EXAMPLES = 128
N_BLK = 8


def shard_levels(stream_key, dims, cuts, smallest, largest):
    gain, own = 1.0, jax.random.fold_in(stream_key, 6)
    for axis_at, shards_of in cuts:
        draws = jnp.exp(jax.random.uniform(jax.random.fold_in(own, axis_at), (shards_of,), jnp.float32, smallest / len(cuts), largest / len(cuts)))
        gain = gain * jnp.repeat(draws, dims[axis_at] // shards_of).reshape([-1 if axis == axis_at else 1 for axis in range(len(dims))])
    return gain


def length_profile(count, total, most, skew):
    weights = [(1 << 20) // math.isqrt(rank ** skew) + 1 for rank in range(2, count + 1)]
    surplus, holding = total - most - (count - 1), [1] * (count - 1)
    while surplus > 0:
        free = [i for i in range(count - 1) if holding[i] < most]
        mass, budget = sum([weights[i] for i in free]), surplus
        for i in free:
            more = min(most - holding[i], max(1, budget * weights[i] // mass), surplus)
            holding[i] = holding[i] + more
            surplus = surplus - more
    return np.array([most] + holding)


def uneven(key, count, total, most, lean):
    if count == 2:
        one = jax.random.randint(key, (), max(1, total - most), min(most, total - 1) + 1)
        return jnp.stack([one, total - one])
    tallies = jnp.asarray(length_profile(count, total, most, lean), jnp.int32)
    pairs = (count - 1) // 2
    source_of, sink = tallies[1:1 + 2 * pairs:2], tallies[2:2 + 2 * pairs:2]
    slack = jnp.minimum(source_of - 1, most - sink)
    shifted = jax.random.randint(jax.random.fold_in(key, 1), (pairs,), 0, 1 << 20) % (slack + 1)
    tallies = tallies.at[1:1 + 2 * pairs:2].set(source_of - shifted).at[2:2 + 2 * pairs:2].set(sink + shifted)
    return tallies[jax.random.permutation(jax.random.fold_in(key, 2), count)]


def bell_draw(key, shape, deviation, limit, cuts=(), held_as=jnp.bfloat16):
    result = jax.random.normal(key, shape, jnp.float32) * deviation
    if len(cuts) > 0:
        result = shard_levels(key, shape, cuts, -0.22, 0.18) * result
    return jnp.clip(result, min=-limit, max=limit).astype(held_as)


def setup_inputs(seed: int = 0) -> dict:
    seeds = jax.random.split(jax.random.key(seed), 10)
    train_act = bell_draw(seeds[0], (TOKENS, D), 0.5, 3.0, ((0, 512),))
    train_grad = bell_draw(seeds[1], (TOKENS, FF), 0.5, 3.0, ((0, 512),))
    query_act = bell_draw(seeds[2], (QTOKENS, D), 0.5, 3.0, ((0, 64), (1, 8)))
    query_grad = bell_draw(seeds[3], (QTOKENS, FF), 0.5, 3.0, ((0, 64),))
    act_basis = bell_draw(seeds[4], (D, BLOCK), BLOCK ** -0.5, 0.25, ((0, 8),))
    grad_basis = bell_draw(seeds[5], (BLOCK, FF), BLOCK ** -0.5, 0.25, ((1, 64),))
    eigenvalues = jnp.clip(jnp.exp(math.log(5.0) - 4.6051702 * jax.random.uniform(seeds[6], (D, FF), jnp.float32) ** shard_levels(seeds[6], (D, FF), ((0, 8), (1, 64)), -0.2, 0.2)), 0.05, 5.0)
    example_ids = jnp.searchsorted(jnp.cumsum(uneven(seeds[7], EXAMPLES, TOKENS, 3 * TOK_DEV * N_BLK // EX_DP, 0)), jnp.arange(TOKENS), side="right").astype(jnp.int32)
    query_ids = jnp.searchsorted(jnp.cumsum(uneven(seeds[8], QUERIES, QTOKENS, 3 * QTOKENS // QUERIES, 0)), jnp.arange(QTOKENS), side="right").astype(jnp.int32)
    return {"train_act": train_act, "train_grad": train_grad, "query_act": query_act, "query_grad": query_grad, "act_basis": act_basis, "grad_basis": grad_basis, "eigenvalues": eigenvalues, "example_ids": example_ids, "query_ids": query_ids}


def round_half(values):
    return lax.optimization_barrier(values.astype(jnp.bfloat16)).astype(jnp.float32)

def reference(train_act, train_grad, query_act, query_grad, act_basis, grad_basis, eigenvalues, example_ids, query_ids):
    highest = lax.Precision.HIGHEST
    count_act = D // BLOCK
    count_grad = FF // BLOCK
    act_blocks = act_basis.astype(jnp.float32).reshape(count_act, BLOCK, BLOCK)
    grad_blocks = grad_basis.astype(jnp.float32).reshape(BLOCK, count_grad, BLOCK)

    def rotate_act(row_data):
        row_count = row_data.shape[0]
        turned = jnp.einsum('tnk,nkl->tnl', row_data.astype(jnp.float32).reshape(row_count, count_act, BLOCK), act_blocks, precision=highest)
        return round_half(turned.reshape(row_count, D))

    def rotate_grad(row_data):
        row_count = row_data.shape[0]
        turned = jnp.einsum('tnk,knl->tnl', row_data.astype(jnp.float32).reshape(row_count, count_grad, BLOCK), grad_blocks, precision=highest)
        return round_half(turned.reshape(row_count, FF))
    act_rot = rotate_act(train_act)
    query_rot = rotate_act(query_act)
    grad_rot = rotate_grad(train_grad)
    query_grad_rot = rotate_grad(query_grad)
    damping = 0.1 * jnp.sum(eigenvalues) / (D * FF)
    norm_scale = float(D * FF) ** (-0.5)
    one_query = (query_ids[:, None] == jnp.arange(QUERIES, dtype=jnp.int32)[None, :]).astype(jnp.float32)
    one_example = (example_ids[:, None] == jnp.arange(EXAMPLES, dtype=jnp.int32)[None, :]).astype(jnp.float32)

    def tile_step(summed, tile_index):
        row_start = tile_index // count_grad * BLOCK
        col_start = tile_index % count_grad * BLOCK
        act_tile = lax.dynamic_slice_in_dim(act_rot, row_start, BLOCK, 1)
        grad_tile = lax.dynamic_slice_in_dim(grad_rot, col_start, BLOCK, 1)
        query_act_tile = lax.dynamic_slice_in_dim(query_rot, row_start, BLOCK, 1)
        query_grad_tile = lax.dynamic_slice_in_dim(query_grad_rot, col_start, BLOCK, 1)
        eigen_tile = lax.dynamic_slice(eigenvalues, (row_start, col_start), (BLOCK, BLOCK))
        weighted = one_query.T[:, :, None] * query_act_tile[None, :, :]
        query_gram = jnp.einsum('qti,tj->qij', weighted, query_grad_tile, precision=highest)
        precond = round_half(query_gram / (eigen_tile[None] + damping) * norm_scale)
        mixed_rows = jnp.einsum('ti,qij->tqj', act_tile, precond, precision=highest)
        token_score = lax.optimization_barrier(jnp.sum(mixed_rows * grad_tile[:, None, :], axis=2))
        return (summed + token_score, None)
    summed, unused = lax.scan(tile_step, jnp.zeros((TOKENS, QUERIES), jnp.float32), jnp.arange(count_act * count_grad, dtype=jnp.int32))
    return jnp.dot(one_example.T, summed, precision=highest)
```

```python
import functools

import jax
import jax.numpy as jnp
import numpy as np
from jax import lax
from jax.experimental import pallas as pl
from jax.experimental.pallas import tpu as pltpu
from jax.sharding import Mesh, PartitionSpec as P

D = 4096
FF = 8192
QUERIES = 16
EXAMPLES = 128
BF = jnp.bfloat16
F32 = jnp.float32
DP = ("zh", "y", "x")
BLK = ("zl", "c")
SIZES = (2, 8, 4, 4, 2)


def swap_all(block, axes):
    return lax.all_to_all(block, axes, split_axis=0, concat_axis=0, tiled=True)


def three_parts(value):
    high = lax.reduce_precision(value, 8, 7)
    rest = value - high
    mid = lax.reduce_precision(rest, 8, 7)
    low = rest - mid
    lane = lax.broadcasted_iota(jnp.int32, (1, 128), 1)
    row = jnp.where(lane == 0, high, jnp.where(lane == 1, mid, jnp.where(lane == 2, low, 0.0)))
    return row.astype(BF)


def score_kernel(
    core, act_own, grad_own, other, queries, act_basis, grad_basis, eigen, ids, query_ids, out, scale, grads
):
    mine = core[0]
    total = 0.0
    for peer in range(8):
        total += jnp.sum(queries[peer, 64:65, :].astype(F32))
    damping = 0.1 * total / (D * FF)
    norm = float(D * FF) ** (-0.5)
    for part in range(4):
        cols = pl.ds(part * 128, 128)
        scale[:, cols] = norm / (eigen[part] + damping)
    basis = act_basis[...]
    columns = jnp.concatenate([grad_basis[part] for part in range(4)], axis=1)

    def rotated(rows, by):
        return jnp.dot(rows, by, preferred_element_type=F32)

    acts = jnp.concatenate(
        [rotated(act_own[...], basis), rotated(other[:, 0:512], basis)], axis=0
    ).astype(BF)
    grads[0:256, :] = rotated(grad_own[...], columns).astype(BF).astype(F32)
    grads[256:512, :] = rotated(other[:, 512:1024], columns).astype(BF).astype(F32)
    query_act = jnp.concatenate([queries[2 * x + mine, 0:64, :] for x in range(4)], axis=0)
    query_grad = jnp.concatenate([queries[2 * x + 1 - mine, 0:64, :] for x in range(4)], axis=0)
    query_turned = rotated(query_act, basis).T.astype(BF)
    query_cols = rotated(query_grad, columns).astype(BF)
    lane = lax.broadcasted_iota(jnp.int32, (512, QUERIES), 1)
    scores = jnp.zeros((512, QUERIES), F32)
    for q in range(QUERIES):
        chosen = (query_ids[...] == q).astype(F32).astype(BF)
        gram = rotated(query_turned * chosen, query_cols)
        precond = (gram * scale[...]).astype(BF)
        mixed = rotated(acts, precond)
        score = jnp.sum(mixed * grads[...], axis=1, keepdims=True)
        scores = jnp.where(lane == q, score, scores)
    row = lax.broadcasted_iota(jnp.int32, (EXAMPLES, 512), 0)
    chosen = (ids[...] == row).astype(F32)
    out[...] = jnp.dot(chosen, scores, precision=lax.Precision.HIGHEST, preferred_element_type=F32)


def shards(
    train_act,
    train_grad,
    query_act,
    query_grad,
    act_basis,
    grad_basis,
    eigenvalues,
    example_ids,
    query_ids,
):
    x = lax.axis_index("x")
    zl = lax.axis_index("zl")
    c = lax.axis_index("c")
    eigen_all = lax.all_gather(eigenvalues, "x", axis=0)
    basis_all = lax.all_gather(grad_basis, "x", axis=0)
    sum_row = three_parts(jnp.sum(eigenvalues))

    acts = jnp.transpose(train_act.reshape(4, 4, 1024), (1, 0, 2))
    cols = jnp.transpose(train_grad.reshape(4, 16, 512), (1, 0, 2))
    query_part = lax.dynamic_index_in_dim(query_grad.reshape(4, 16, 4, 128), zl, 2, keepdims=False)
    query_part = jnp.transpose(query_part, (1, 0, 2))
    wide = (16, 4, 4)
    message = jnp.concatenate(
        [
            jnp.broadcast_to(acts[None], wide + (1024,)),
            jnp.broadcast_to(cols[:, None], wide + (512,)),
            jnp.broadcast_to(query_act[None, None], wide + (512,)),
            jnp.broadcast_to(query_part[:, None], wide + (128,)),
            jnp.broadcast_to(sum_row[None, None], wide + (128,)),
        ],
        axis=3,
    ).reshape(64, 4, 2304)
    got = swap_all(message, ("zh", "y", "zl"))

    pair = got[:, :, 0:1024].reshape(64, 4, 2, 512)
    act_own = lax.dynamic_index_in_dim(pair, c, 2, keepdims=False).reshape(256, 512)
    act_away = lax.dynamic_index_in_dim(pair, 1 - c, 2, keepdims=False).reshape(256, 512)
    grad_own = got[:, :, 1024:1536].reshape(256, 512)
    other = lax.ppermute(jnp.concatenate([act_away, grad_own], axis=1), "c", [(0, 1), (1, 0)])

    by_zl = got.reshape(16, 4, 4, 2304)
    query_rows = lax.dynamic_index_in_dim(by_zl, zl, 1, keepdims=False)[:, :, 1536:2048].reshape(64, 512)
    query_cols = jnp.transpose(by_zl[:, :, :, 2048:2176], (0, 2, 1, 3)).reshape(64, 512)
    partial = three_parts(jnp.sum(got[:, 0, 2176:2304].astype(F32)))
    partial = jnp.pad(partial, ((0, 7), (0, 384)))
    to_same = jnp.concatenate([query_rows, partial], axis=0)
    to_other = jnp.concatenate([query_cols, partial], axis=0)
    first = jnp.where(c == 0, to_same, to_other)
    second = jnp.where(c == 0, to_other, to_same)
    queries = jnp.broadcast_to(jnp.stack([first, second])[None], (4, 2, 72, 512)).reshape(8, 72, 512)
    queries = swap_all(queries, ("x", "c"))

    ids = lax.dynamic_index_in_dim(example_ids.reshape(16, 4, 4, 2, 4), x, 1, keepdims=False)
    ids_own = lax.dynamic_index_in_dim(ids, c, 2, keepdims=False).reshape(1, 256)
    ids_other = lax.dynamic_index_in_dim(ids, 1 - c, 2, keepdims=False).reshape(1, 256)
    ids = jnp.concatenate([ids_own, ids_other], axis=1)
    ids = (ids % 64) // 2 * 4 + ids // 64 * 2 + ids % 2
    query_order = jnp.transpose(query_ids.reshape(16, 4, 4), (1, 0, 2)).reshape(1, 256)

    vmem = pl.BlockSpec(memory_space=pltpu.VMEM)
    partial_scores = pl.pallas_call(
        score_kernel,
        out_shape=jax.ShapeDtypeStruct((EXAMPLES, QUERIES), F32),
        in_specs=[pl.BlockSpec(memory_space=pltpu.SMEM)] + [vmem] * 9,
        out_specs=vmem,
        scratch_shapes=[pltpu.VMEM((512, 512), F32), pltpu.VMEM((512, 512), F32)],
        compiler_params=pltpu.CompilerParams(vmem_limit_bytes=40 << 20),
    )(
        c.reshape(1).astype(jnp.int32),
        act_own,
        grad_own,
        other,
        queries,
        act_basis,
        basis_all,
        eigen_all,
        ids,
        query_order,
    )
    got = swap_all(partial_scores.reshape(32, 4, 16), ("y", "x"))
    sums = jnp.sum(got, axis=0).reshape(2, 1, 2, 16)
    got = swap_all(jnp.broadcast_to(sums, (2, 8, 2, 16)).reshape(16, 2, 16), ("zh", "zl", "c"))
    return jnp.sum(got, axis=0)


def solution(mesh):
    fine = Mesh(np.asarray(mesh.devices).reshape(SIZES), DP + BLK)
    placed = (
        P(DP + BLK, None),
        P(DP + BLK, None),
        P(DP, BLK),
        P(DP, None),
        P(BLK, None),
        P(None, DP),
        P(BLK, DP),
        P(),
        P(),
    )
    return jax.shard_map(
        shards, mesh=fine, in_specs=placed, out_specs=P(DP, None), check_vma=False
    )
```

```python
import jax
import jax.numpy as jnp
import numpy as np
from jax import lax
from jax.experimental import pallas as pl
from jax.experimental.pallas import tpu as pltpu
from jax.sharding import Mesh, PartitionSpec as P

D = 4096
FF = 8192
QUERIES = 16
EXAMPLES = 128
BF = jnp.bfloat16
F32 = jnp.float32
DP = ("zh", "y", "x")
BLK = ("zl", "c")
SIZES = (2, 8, 4, 4, 2)


def swap_all(block, axes):
    return lax.all_to_all(block, axes, split_axis=0, concat_axis=0, tiled=True)


def three_parts(rows):
    high = rows.astype(BF).astype(F32)
    rest = rows - high
    mid = rest.astype(BF).astype(F32)
    return high, mid, rest - mid


def pack_kernel(place, act, grad, query_act, query_grad, eigen, out):
    zl, c = place[0], place[1]
    sums = jnp.sum(jnp.sum(eigen[...].reshape(64, 8, 128), axis=0), axis=0, keepdims=True)
    sums = jnp.concatenate([*three_parts(sums), jnp.zeros((1, 128), F32)], axis=0).astype(BF)
    for z in range(4):
        own = act[:, pl.ds(pl.multiple_of(z * 1024 + c * 512, 128), 512)]
        away = act[:, pl.ds(pl.multiple_of(z * 1024 + 512 - c * 512, 128), 512)]
        for m in range(16):
            to = m * 4 + z
            for t in range(4):
                part = slice(t * 128, t * 128 + 128)
                cols = slice(m * 512 + t * 128, m * 512 + t * 128 + 128)
                out[to, t] = own[:, part]
                out[to, 4 + t] = away[:, part]
                out[to, 8 + t] = grad[:, cols]
                out[to, 12 + t] = query_grad[:, cols]
            out[to, 16] = sums
    for m in range(16):
        for t in range(4):
            out[m * 4 + zl, 12 + t] = query_act[:, t * 128 : t * 128 + 128]


def relay_kernel(place, got, out):
    zl, c = place[0], place[1]
    sums = jnp.sum(jnp.sum(got[:, 16].astype(F32), axis=0), axis=0, keepdims=True)
    sums = jnp.concatenate([*three_parts(sums), jnp.zeros((5, 128), F32)], axis=0).astype(BF)
    for core in range(2):
        source = zl + jnp.where(c == core, 0, 1 - 2 * (zl % 2))
        for t in range(4):
            for s in range(16):
                out[core, t * 64 + s * 4 : t * 64 + s * 4 + 4, :] = got[s * 4 + source, 12 + t]
        out[core, 256:264, :] = sums
        for x in range(1, 4):
            out[2 * x + core] = out[core]


def score_kernel(
    place, own, other, queries, act_basis, basis0, basis1, basis2, basis3, eigen, ids, query_ids, out,
    scale, columns, grads
):
    c, x = place[1], place[2]
    total = 0.0
    for peer in range(8):
        total += jnp.sum(queries[peer, 256:264, :].astype(F32))
    damping = 0.1 * total / (D * FF)
    norm = float(D * FF) ** (-0.5)
    for part in range(4):
        scale[:, part * 128 : part * 128 + 128] = norm / (eigen[part] + damping)
    for step, part in enumerate((basis0, basis1, basis2, basis3)):
        at = pl.multiple_of(lax.rem(x + 4 - step, 4) * 128, 128)
        columns[:, pl.ds(at, 128)] = part[...]
    basis = act_basis[...]

    def rotated(rows, by):
        return jnp.dot(rows, by, preferred_element_type=F32)

    def tiles(ref, first):
        return jnp.concatenate([ref[first + t] for t in range(4)], axis=1)

    def query_rows(core):
        rows = [
            jnp.concatenate([queries[2 * p + core, t * 64 : t * 64 + 64, :] for t in range(4)], axis=1)
            for p in range(4)
        ]
        return jnp.concatenate(rows, axis=0)

    acts = jnp.concatenate([rotated(tiles(own, 0), basis), rotated(tiles(other, 0), basis)], axis=0)
    acts = acts.astype(BF)
    grads[0:256, :] = rotated(tiles(own, 8), columns[...]).astype(BF).astype(F32)
    grads[256:512, :] = rotated(tiles(other, 4), columns[...]).astype(BF).astype(F32)
    query_turned = rotated(query_rows(c), basis).T.astype(BF)
    query_cols = rotated(query_rows(1 - c), columns[...]).astype(BF)
    lane = lax.broadcasted_iota(jnp.int32, (512, QUERIES), 1)
    scores = jnp.zeros((512, QUERIES), F32)
    for q in range(QUERIES):
        chosen = (query_ids[...] == q).astype(F32).astype(BF)
        gram = rotated(query_turned * chosen, query_cols)
        precond = (gram * scale[...]).astype(BF)
        mixed = rotated(acts, precond)
        score = jnp.sum(mixed * grads[...], axis=1, keepdims=True)
        scores = jnp.where(lane == q, score, scores)
    row = lax.broadcasted_iota(jnp.int32, (EXAMPLES, 512), 0)
    chosen = (ids[...] == row).astype(F32)
    out[...] = jnp.dot(chosen, scores, precision=lax.Precision.HIGHEST, preferred_element_type=F32)


def local_call(kernel, out_shape, dtype, place, arrays, scratch=()):
    vmem = pl.BlockSpec(memory_space=pltpu.VMEM)
    return pl.pallas_call(
        kernel,
        out_shape=jax.ShapeDtypeStruct(out_shape, dtype),
        in_specs=[pl.BlockSpec(memory_space=pltpu.SMEM)] + [vmem] * len(arrays),
        out_specs=vmem,
        scratch_shapes=list(scratch),
        compiler_params=pltpu.CompilerParams(vmem_limit_bytes=40 << 20),
    )(place, *arrays)


def shards(
    train_act,
    train_grad,
    query_act,
    query_grad,
    act_basis,
    grad_basis,
    eigenvalues,
    example_ids,
    query_ids,
):
    x = lax.axis_index("x")
    c = lax.axis_index("c")
    place = jnp.stack([lax.axis_index("zl"), c, x]).astype(jnp.int32)

    message = local_call(
        pack_kernel, (64, 17, 4, 128), BF, place, (train_act, train_grad, query_act, query_grad, eigenvalues)
    )
    message, eigenvalues, grad_basis = lax.optimization_barrier((message, eigenvalues, grad_basis))
    eigen_all = lax.all_gather(eigenvalues, "x", axis=0)
    bases = [lax.ppermute(grad_basis, "x", [(p, (p + step) % 4) for p in range(4)]) for step in (1, 2, 3)]
    got = swap_all(message, ("zh", "y", "zl"))

    ids = lax.dynamic_index_in_dim(example_ids.reshape(16, 4, 4, 2, 4), x, 1, keepdims=False)
    ids_own = lax.dynamic_index_in_dim(ids, c, 2, keepdims=False).reshape(1, 256)
    ids_other = lax.dynamic_index_in_dim(ids, 1 - c, 2, keepdims=False).reshape(1, 256)
    ids = jnp.concatenate([ids_own, ids_other], axis=1)
    ids = (ids % 64) // 2 * 4 + ids // 64 * 2 + ids % 2
    query_order = jnp.transpose(query_ids.reshape(16, 4, 4), (1, 0, 2)).reshape(1, 256)
    got, bases, ids, query_order = lax.optimization_barrier((got, bases, ids, query_order))

    queries = local_call(relay_kernel, (8, 264, 128), BF, place, (got,))
    queries = swap_all(queries, ("x", "c"))
    own = jnp.transpose(got[:, 0:12], (1, 0, 2, 3)).reshape(12, 256, 128)
    other = lax.ppermute(own[4:12], "c", [(0, 1), (1, 0)])

    partial_scores = local_call(
        score_kernel,
        (EXAMPLES, QUERIES),
        F32,
        place,
        (own, other, queries, act_basis, grad_basis, *bases, eigen_all, ids, query_order),
        (pltpu.VMEM((512, 512), F32), pltpu.VMEM((512, 512), BF), pltpu.VMEM((512, 512), F32)),
    )
    got = swap_all(partial_scores.reshape(32, 4, 16), ("y", "x"))
    sums = jnp.sum(got, axis=0).reshape(2, 1, 2, 16)
    got = swap_all(jnp.broadcast_to(sums, (2, 8, 2, 16)).reshape(16, 2, 16), ("zh", "zl", "c"))
    return jnp.sum(got, axis=0)


def solution(mesh):
    fine = Mesh(np.asarray(mesh.devices).reshape(SIZES), DP + BLK)
    placed = (
        P(DP + BLK, None),
        P(DP + BLK, None),
        P(DP, BLK),
        P(DP, None),
        P(BLK, None),
        P(None, DP),
        P(BLK, DP),
        P(),
        P(),
    )
    return jax.shard_map(
        shards, mesh=fine, in_specs=placed, out_specs=P(DP, None), check_vma=False
    )
```

```python
import jax
import jax.numpy as jnp
import numpy as np
from jax import lax
from jax.experimental import pallas as pl
from jax.experimental.pallas import tpu as pltpu
from jax.sharding import Mesh, PartitionSpec as P

D = 4096
FF = 8192
QUERIES = 16
EXAMPLES = 128
BF = jnp.bfloat16
F32 = jnp.float32
DP = ("zh", "y", "x")
BLK = ("zl", "c")
SIZES = (2, 8, 4, 4, 2)


def swap_all(block, axes):
    return lax.all_to_all(block, axes, split_axis=0, concat_axis=0, tiled=True)


def three_parts(rows):
    high = rows.astype(BF).astype(F32)
    rest = rows - high
    mid = rest.astype(BF).astype(F32)
    return high, mid, rest - mid


def pack_kernel(copies, act, grad, query_act, query_grad, eigen, out):
    zl, c = lax.axis_index("zl"), lax.axis_index("c")
    for copy in copies:
        copy.wait()
    sums = jnp.sum(jnp.sum(eigen[...].reshape(64, 8, 128), axis=0), axis=0, keepdims=True)
    sums = jnp.concatenate([*three_parts(sums), jnp.zeros((1, 128), F32)], axis=0).astype(BF)
    for z in range(4):
        own = act[:, pl.ds(pl.multiple_of(z * 1024 + c * 512, 128), 512)]
        away = act[:, pl.ds(pl.multiple_of(z * 1024 + 512 - c * 512, 128), 512)]
        for m in range(16):
            to = m * 4 + z
            for t in range(4):
                part = slice(t * 128, t * 128 + 128)
                cols = slice(m * 512 + t * 128, m * 512 + t * 128 + 128)
                out[to, t] = own[:, part]
                out[to, 4 + t] = away[:, part]
                out[to, 8 + t] = grad[:, cols]
                out[to, 12 + t] = query_grad[:, cols]
            out[to, 16] = sums
    for m in range(16):
        for t in range(4):
            out[m * 4 + zl, 12 + t] = query_act[:, t * 128 : t * 128 + 128]


def relay_kernel(copies, got, out):
    zl, c = lax.axis_index("zl"), lax.axis_index("c")
    sums = jnp.sum(jnp.sum(got[:, 16].astype(F32), axis=0), axis=0, keepdims=True)
    sums = jnp.concatenate([*three_parts(sums), jnp.zeros((5, 128), F32)], axis=0).astype(BF)
    for core in range(2):
        source = zl + jnp.where(c == core, 0, 1 - 2 * (zl % 2))
        for t in range(4):
            for s in range(16):
                out[core, t * 64 + s * 4 : t * 64 + s * 4 + 4, :] = got[s * 4 + source, 12 + t]
        out[core, 256:264, :] = sums
        for x in range(1, 4):
            out[2 * x + core] = out[core]


def rotated(rows, by):
    return jnp.dot(rows, by, preferred_element_type=F32)


def ring_slot(x, step):
    return pl.multiple_of(lax.rem(x + 4 - step, 4) * 128, 128)


def turn_kernel(copies, own, other, act_basis, basis0, basis1, basis2, basis3, acts, grads, columns):
    x = lax.axis_index("x")
    for copy in copies:
        copy.wait()
    for step, part in enumerate((basis0, basis1, basis2, basis3)):
        columns[:, pl.ds(ring_slot(x, step), 128)] = part[...]

    def tiles(ref, first):
        return jnp.concatenate([ref[first + t] for t in range(4)], axis=1)

    acts[0:256, :] = rotated(tiles(own, 0), act_basis[...]).astype(BF)
    acts[256:512, :] = rotated(tiles(other, 0), act_basis[...]).astype(BF)
    grads[0:256, :] = rotated(tiles(own, 8), columns[...]).astype(BF).astype(F32)
    grads[256:512, :] = rotated(tiles(other, 4), columns[...]).astype(BF).astype(F32)


def score_kernel(
    copies, acts, grads, columns, queries, act_basis, ids, query_ids, eigen0, eigen1, eigen2, eigen3, out, scale
):
    c, x = lax.axis_index("c"), lax.axis_index("x")
    for copy in copies:
        copy.wait()
    total = 0.0
    for peer in range(8):
        total += jnp.sum(queries[peer, 256:264, :].astype(F32))
    damping = 0.1 * total / (D * FF)
    norm = float(D * FF) ** (-0.5)
    for step, part in enumerate((eigen0, eigen1, eigen2, eigen3)):
        scale[:, pl.ds(ring_slot(x, step), 128)] = norm / (part[...] + damping)

    def query_rows(core):
        rows = [
            jnp.concatenate([queries[2 * p + core, t * 64 : t * 64 + 64, :] for t in range(4)], axis=1)
            for p in range(4)
        ]
        return jnp.concatenate(rows, axis=0)

    query_turned = rotated(query_rows(c), act_basis[...]).T.astype(BF)
    query_cols = rotated(query_rows(1 - c), columns[...]).astype(BF)
    lane = lax.broadcasted_iota(jnp.int32, (512, QUERIES), 1)
    scores = jnp.zeros((512, QUERIES), F32)
    for q in range(QUERIES):
        chosen = (query_ids[...] == q).astype(F32).astype(BF)
        gram = rotated(query_turned * chosen, query_cols)
        precond = (gram * scale[...]).astype(BF)
        mixed = rotated(acts[...], precond)
        score = jnp.sum(mixed * grads[...], axis=1, keepdims=True)
        scores = jnp.where(lane == q, score, scores)
    row = lax.broadcasted_iota(jnp.int32, (EXAMPLES, 512), 0)
    chosen = (ids[...] == row).astype(F32)
    out[...] = jnp.dot(chosen, scores, precision=lax.Precision.HIGHEST, preferred_element_type=F32)


def local_call(kernel, mib, outs, near, far, scratch=()):
    count = len(far)

    def body(*refs):
        refs = list(refs)
        held, refs = refs[: len(near)], refs[len(near) :]
        sources, refs = refs[:count], refs[count:]
        results, refs = refs[: len(outs)], refs[len(outs) :]
        buffers, refs = refs[:count], refs[count:]
        copies = []
        if count:
            done, refs = refs[0], refs[1:]
            copies = [pltpu.make_async_copy(sources[k], buffers[k], done.at[k]) for k in range(count)]
        for copy in copies:
            copy.start()
        kernel(copies, *held, *buffers, *results, *refs)

    staged = [pltpu.VMEM(array.shape, array.dtype) for array in far]
    if count:
        staged.append(pltpu.SemaphoreType.DMA((count,)))
    vmem = pl.BlockSpec(memory_space=pltpu.VMEM)
    arrays = [pltpu.with_memory_space_constraint(array, pltpu.VMEM) for array in near]
    arrays += [pltpu.with_memory_space_constraint(array, pltpu.HBM) for array in far]
    return pl.pallas_call(
        body,
        out_shape=[jax.ShapeDtypeStruct(shape, dtype) for shape, dtype in outs],
        in_specs=[vmem] * len(near) + [pl.BlockSpec(memory_space=pltpu.HBM)] * count,
        out_specs=[vmem] * len(outs),
        scratch_shapes=staged + list(scratch),
        compiler_params=pltpu.CompilerParams(vmem_limit_bytes=mib << 20),
        cost_estimate=pl.CostEstimate(flops=1000, transcendentals=0, bytes_accessed=1000),
    )(*arrays)


def ring_parts(block):
    return [block] + [
        lax.ppermute(block, "x", [(p, (p + step) % 4) for p in range(4)]) for step in (1, 2, 3)
    ]


def shards(
    train_act,
    train_grad,
    query_act,
    query_grad,
    act_basis,
    grad_basis,
    eigenvalues,
    example_ids,
    query_ids,
):
    x = lax.axis_index("x")
    c = lax.axis_index("c")
    (message,) = local_call(
        pack_kernel,
        6,
        [((64, 17, 4, 128), BF)],
        (),
        (train_act, train_grad, query_act, query_grad, eigenvalues),
    )
    message, eigenvalues, grad_basis = lax.optimization_barrier((message, eigenvalues, grad_basis))
    eigens = ring_parts(eigenvalues)
    bases = ring_parts(grad_basis)
    got = swap_all(message, ("zh", "y", "zl"))

    ids = lax.dynamic_index_in_dim(example_ids.reshape(16, 4, 4, 2, 4), x, 1, keepdims=False)
    ids_own = lax.dynamic_index_in_dim(ids, c, 2, keepdims=False).reshape(1, 256)
    ids_other = lax.dynamic_index_in_dim(ids, 1 - c, 2, keepdims=False).reshape(1, 256)
    ids = jnp.concatenate([ids_own, ids_other], axis=1)
    ids = (ids % 64) // 2 * 4 + ids // 64 * 2 + ids % 2
    query_order = jnp.transpose(query_ids.reshape(16, 4, 4), (1, 0, 2)).reshape(1, 256)
    got, eigens, bases, ids, query_order = lax.optimization_barrier((got, eigens, bases, ids, query_order))

    (queries,) = local_call(relay_kernel, 6, [((8, 264, 128), BF)], (got,), ())
    queries, got = lax.optimization_barrier((queries, got))
    queries = swap_all(queries, ("x", "c"))
    own = jnp.transpose(got[:, 0:12], (1, 0, 2, 3)).reshape(12, 256, 128)
    other = lax.ppermute(own[4:12], "c", [(0, 1), (1, 0)])
    acts, grads, columns = local_call(
        turn_kernel,
        12,
        [((512, 512), BF), ((512, 512), F32), ((512, 512), BF)],
        (own, other),
        (act_basis, *bases),
    )
    (partial_scores,) = local_call(
        score_kernel,
        20,
        [((EXAMPLES, QUERIES), F32)],
        (acts, grads, columns, queries),
        (act_basis, ids, query_order, *eigens),
        (pltpu.VMEM((512, 512), F32),),
    )
    got = swap_all(partial_scores.reshape(32, 4, 16), ("y", "x"))
    sums = jnp.sum(got, axis=0).reshape(2, 1, 2, 16)
    got = swap_all(jnp.broadcast_to(sums, (2, 8, 2, 16)).reshape(16, 2, 16), ("zh", "zl", "c"))
    return jnp.sum(got, axis=0)


def solution(mesh):
    fine = Mesh(np.asarray(mesh.devices).reshape(SIZES), DP + BLK)
    placed = (
        P(DP + BLK, None),
        P(DP + BLK, None),
        P(DP, BLK),
        P(DP, None),
        P(BLK, None),
        P(None, DP),
        P(BLK, DP),
        P(),
        P(),
    )
    return jax.shard_map(
        shards, mesh=fine, in_specs=placed, out_specs=P(DP, None), check_vma=False
    )
```

```python
import jax
import jax.numpy as jnp
import numpy as np
from jax import lax
from jax.experimental import pallas as pl
from jax.experimental.pallas import tpu as pltpu
from jax.sharding import Mesh, PartitionSpec as P

D = 4096
FF = 8192
QUERIES = 16
EXAMPLES = 128
BF = jnp.bfloat16
F32 = jnp.float32
DP = ("zh", "y", "x")
BLK = ("zl", "c")
SIZES = (2, 8, 4, 4, 2)


def swap_all(block, axes):
    return lax.all_to_all(block, axes, split_axis=0, concat_axis=0, tiled=True)


def three_parts(rows):
    high = rows.astype(BF).astype(F32)
    rest = rows - high
    mid = rest.astype(BF).astype(F32)
    return high, mid, rest - mid


def pack_kernel(copies, act, grad, query_act, query_grad, eigen, out):
    zl, c = lax.axis_index("zl"), lax.axis_index("c")
    for copy in copies:
        copy.wait()
    sums = jnp.sum(jnp.sum(eigen[...].reshape(64, 8, 128), axis=0), axis=0, keepdims=True)
    sums = jnp.concatenate([*three_parts(sums), jnp.zeros((1, 128), F32)], axis=0).astype(BF)
    for z in range(4):
        own = act[:, pl.ds(pl.multiple_of(z * 1024 + c * 512, 128), 512)]
        away = act[:, pl.ds(pl.multiple_of(z * 1024 + 512 - c * 512, 128), 512)]
        for m in range(16):
            to = m * 4 + z
            for t in range(4):
                part = slice(t * 128, t * 128 + 128)
                cols = slice(m * 512 + t * 128, m * 512 + t * 128 + 128)
                out[to, t] = own[:, part]
                out[to, 4 + t] = away[:, part]
                out[to, 8 + t] = grad[:, cols]
                out[to, 12 + t] = query_grad[:, cols]
            out[to, 16] = sums
    for m in range(16):
        for t in range(4):
            out[m * 4 + zl, 12 + t] = query_act[:, t * 128 : t * 128 + 128]


def relay_kernel(copies, got, out):
    zl, c = lax.axis_index("zl"), lax.axis_index("c")
    sums = jnp.sum(jnp.sum(got[:, 16].astype(F32), axis=0), axis=0, keepdims=True)
    sums = jnp.concatenate([*three_parts(sums), jnp.zeros((5, 128), F32)], axis=0).astype(BF)
    for core in range(2):
        source = zl + jnp.where(c == core, 0, 1 - 2 * (zl % 2))
        for t in range(4):
            for s in range(16):
                out[core, t * 64 + s * 4 : t * 64 + s * 4 + 4, :] = got[s * 4 + source, 12 + t]
        out[core, 256:264, :] = sums
        for x in range(1, 4):
            out[2 * x + core] = out[core]


def rotated(rows, by):
    return jnp.dot(rows, by, preferred_element_type=F32)


def ring_slot(x, step):
    return pl.multiple_of(lax.rem(x + 4 - step, 4) * 128, 128)


def turn_kernel(
    copies, own, other, act_basis, basis0, basis1, basis2, basis3, eigen0, eigen1, eigen2, eigen3,
    acts, grads, columns, eigen
):
    x = lax.axis_index("x")
    for copy in copies:
        copy.wait()
    for step, part in enumerate((basis0, basis1, basis2, basis3)):
        columns[:, pl.ds(ring_slot(x, step), 128)] = part[...]
    for step, part in enumerate((eigen0, eigen1, eigen2, eigen3)):
        eigen[:, pl.ds(ring_slot(x, step), 128)] = part[...]

    def tiles(ref, first):
        return jnp.concatenate([ref[first + t] for t in range(4)], axis=1)

    acts[0:256, :] = rotated(tiles(own, 0), act_basis[...]).astype(BF)
    acts[256:512, :] = rotated(tiles(other, 0), act_basis[...]).astype(BF)
    grads[0:256, :] = rotated(tiles(own, 8), columns[...]).astype(BF)
    grads[256:512, :] = rotated(tiles(other, 4), columns[...]).astype(BF)


def score_kernel(
    copies, acts, grads_in, columns, eigen, queries, act_basis, query_ids, ids, out, scale, grads
):
    c = lax.axis_index("c")
    total = 0.0
    for peer in range(8):
        total += jnp.sum(queries[peer, 256:264, :].astype(F32))
    damping = 0.1 * total / (D * FF)
    norm = float(D * FF) ** (-0.5)
    scale[...] = norm / (eigen[...] + damping)
    grads[...] = grads_in[...].astype(F32)

    def query_rows(core):
        rows = [
            jnp.concatenate([queries[2 * p + core, t * 64 : t * 64 + 64, :] for t in range(4)], axis=1)
            for p in range(4)
        ]
        return jnp.concatenate(rows, axis=0)

    for copy in copies:
        copy.wait()
    query_turned = rotated(query_rows(c), act_basis[...]).T.astype(BF)
    query_cols = rotated(query_rows(1 - c), columns[...]).astype(BF)
    lane = lax.broadcasted_iota(jnp.int32, (512, QUERIES), 1)
    scores = jnp.zeros((512, QUERIES), F32)
    for q in range(QUERIES):
        chosen = (query_ids[...] == q).astype(F32).astype(BF)
        gram = rotated(query_turned * chosen, query_cols)
        precond = (gram * scale[...]).astype(BF)
        mixed = rotated(acts[...], precond)
        score = jnp.sum(mixed * grads[...], axis=1, keepdims=True)
        scores = jnp.where(lane == q, score, scores)
    row = lax.broadcasted_iota(jnp.int32, (EXAMPLES, 512), 0)
    chosen = (ids[...] == row).astype(F32)
    sums = jnp.dot(chosen, scores, precision=lax.Precision.HIGHEST, preferred_element_type=F32)
    sums = [sums[part * 32 : part * 32 + 32, :] for part in range(4)]
    out[...] = jnp.concatenate(sums + [jnp.zeros((32, 64), F32)], axis=1)


def local_call(kernel, mib, outs, near, far, scratch=()):
    count = len(far)

    def body(*refs):
        refs = list(refs)
        held, refs = refs[: len(near)], refs[len(near) :]
        sources, refs = refs[:count], refs[count:]
        results, refs = refs[: len(outs)], refs[len(outs) :]
        buffers, refs = refs[:count], refs[count:]
        copies = []
        if count:
            done, refs = refs[0], refs[1:]
            copies = [pltpu.make_async_copy(sources[k], buffers[k], done.at[k]) for k in range(count)]
        for copy in copies:
            copy.start()
        kernel(copies, *held, *buffers, *results, *refs)

    staged = [pltpu.VMEM(array.shape, array.dtype) for array in far]
    if count:
        staged.append(pltpu.SemaphoreType.DMA((count,)))
    vmem = pl.BlockSpec(memory_space=pltpu.VMEM)
    arrays = [pltpu.with_memory_space_constraint(array, pltpu.VMEM) for array in near]
    arrays += [pltpu.with_memory_space_constraint(array, pltpu.HBM) for array in far]
    return pl.pallas_call(
        body,
        out_shape=[jax.ShapeDtypeStruct(shape, dtype) for shape, dtype in outs],
        in_specs=[vmem] * len(near) + [pl.BlockSpec(memory_space=pltpu.HBM)] * count,
        out_specs=[vmem] * len(outs),
        scratch_shapes=staged + list(scratch),
        compiler_params=pltpu.CompilerParams(vmem_limit_bytes=mib << 20),
        cost_estimate=pl.CostEstimate(flops=1000, transcendentals=0, bytes_accessed=1000),
    )(*arrays)


def ring_parts(block, way):
    def moved(part, step):
        return lax.ppermute(part, "x", [(p, (p + step) % 4) for p in range(4)])

    one, three = moved(block, 1), moved(block, 3)
    return [block, one, moved(one, 1) if way == 1 else moved(three, 3), three]


def shards(
    train_act,
    train_grad,
    query_act,
    query_grad,
    act_basis,
    grad_basis,
    eigenvalues,
    example_ids,
    query_ids,
):
    x = lax.axis_index("x")
    c = lax.axis_index("c")
    (message,) = local_call(
        pack_kernel,
        6,
        [((64, 17, 4, 128), BF)],
        (),
        (train_act, train_grad, query_act, query_grad, eigenvalues),
    )
    message, eigenvalues, grad_basis = lax.optimization_barrier((message, eigenvalues, grad_basis))
    eigens = ring_parts(eigenvalues, 3)
    bases = ring_parts(grad_basis, 1)
    got = swap_all(message, ("zh", "y", "zl"))

    ids = lax.dynamic_index_in_dim(example_ids.reshape(16, 4, 4, 2, 4), x, 1, keepdims=False)
    ids_own = lax.dynamic_index_in_dim(ids, c, 2, keepdims=False).reshape(1, 256)
    ids_other = lax.dynamic_index_in_dim(ids, 1 - c, 2, keepdims=False).reshape(1, 256)
    ids = jnp.concatenate([ids_own, ids_other], axis=1)
    ids = ids // 64 * 64 + ids % 2 * 32 + ids % 64 // 2
    query_order = jnp.transpose(query_ids.reshape(16, 4, 4), (1, 0, 2)).reshape(1, 256)
    got, eigens, bases, ids, query_order = lax.optimization_barrier((got, eigens, bases, ids, query_order))

    (queries,) = local_call(relay_kernel, 6, [((8, 264, 128), BF)], (got,), ())
    queries, got = lax.optimization_barrier((queries, got))
    queries = swap_all(queries, ("x", "c"))
    other = lax.ppermute(got, "c", [(0, 1), (1, 0)])
    own = jnp.transpose(got[:, 0:12], (1, 0, 2, 3)).reshape(12, 256, 128)
    other = jnp.transpose(other[:, 4:12], (1, 0, 2, 3)).reshape(8, 256, 128)
    held = local_call(
        turn_kernel,
        12,
        [((512, 512), BF), ((512, 512), BF), ((512, 512), BF), ((512, 512), F32)],
        (own, other),
        (act_basis, *bases, *eigens),
    )
    (partial_scores,) = local_call(
        score_kernel,
        20,
        [((32, 128), F32)],
        (*held, queries),
        (act_basis, query_order, ids),
        (pltpu.VMEM((512, 512), F32), pltpu.VMEM((512, 512), F32)),
    )
    sums = jnp.sum(swap_all(partial_scores, ("y", "x")), axis=0, keepdims=True)
    sums = jnp.sum(swap_all(jnp.broadcast_to(sums, (16, 128)), ("zh", "zl", "c")), axis=0)
    return lax.dynamic_slice_in_dim(sums, lax.axis_index("zh") * 32, 32, 0).reshape(2, 16)


def solution(mesh):
    fine = Mesh(np.asarray(mesh.devices).reshape(SIZES), DP + BLK)
    placed = (
        P(DP + BLK, None),
        P(DP + BLK, None),
        P(DP, BLK),
        P(DP, None),
        P(BLK, None),
        P(None, DP),
        P(BLK, DP),
        P(),
        P(),
    )
    return jax.shard_map(
        shards, mesh=fine, in_specs=placed, out_specs=P(DP, None), check_vma=False
    )
```

```python
import jax
import jax.numpy as jnp
import numpy as np
from jax import lax
from jax.experimental import pallas as pl
from jax.experimental.pallas import tpu as pltpu
from jax.sharding import Mesh, PartitionSpec as P

D = 4096
FF = 8192
QUERIES = 16
EXAMPLES = 128
BF = jnp.bfloat16
F32 = jnp.float32
DP = ("zh", "y", "x")
BLK = ("zl", "c")
SIZES = (2, 8, 4, 4, 2)


def swap_all(block, axes):
    return lax.all_to_all(block, axes, split_axis=0, concat_axis=0, tiled=True)


def three_parts(rows):
    high = rows.astype(BF).astype(F32)
    rest = rows - high
    mid = rest.astype(BF).astype(F32)
    return high, mid, rest - mid


def pack_kernel(copies, act, grad, query_act, query_grad, eigen, out):
    zl, c = lax.axis_index("zl"), lax.axis_index("c")
    for copy in copies:
        copy.wait()
    sums = jnp.sum(jnp.sum(eigen[...].reshape(64, 8, 128), axis=0), axis=0, keepdims=True)
    sums = jnp.concatenate([*three_parts(sums), jnp.zeros((1, 128), F32)], axis=0).astype(BF)
    for z in range(4):
        own = act[:, pl.ds(pl.multiple_of(z * 1024 + c * 512, 128), 512)]
        away = act[:, pl.ds(pl.multiple_of(z * 1024 + 512 - c * 512, 128), 512)]
        for k in range(16):
            to, m = k * 4 + z, k % 2 * 8 + k // 2
            for t in range(4):
                part = slice(t * 128, t * 128 + 128)
                cols = slice(m * 512 + t * 128, m * 512 + t * 128 + 128)
                out[to, t] = own[:, part]
                out[to, 4 + t] = away[:, part]
                out[to, 8 + t] = grad[:, cols]
                out[to, 12 + t] = query_grad[:, cols]
            out[to, 16] = sums
    for m in range(16):
        for t in range(4):
            out[m * 4 + zl, 12 + t] = query_act[:, t * 128 : t * 128 + 128]


def relay_kernel(copies, got, out):
    zl, c = lax.axis_index("zl"), lax.axis_index("c")
    sums = jnp.sum(jnp.sum(got[:, 16].astype(F32), axis=0), axis=0, keepdims=True)
    sums = jnp.concatenate([*three_parts(sums), jnp.zeros((5, 128), F32)], axis=0).astype(BF)
    for core in range(2):
        source = zl + jnp.where(c == core, 0, 1 - 2 * (zl % 2))
        for t in range(4):
            for s in range(16):
                out[4 * core, t * 64 + s * 4 : t * 64 + s * 4 + 4, :] = got[s * 4 + source, 12 + t]
        out[4 * core, 256:264, :] = sums
        for x in range(1, 4):
            out[4 * core + x] = out[4 * core]


def rotated(rows, by):
    return jnp.dot(rows, by, preferred_element_type=F32)


def ring_slot(x, step):
    return pl.multiple_of(lax.rem(x + 4 - step, 4) * 128, 128)


def turn_kernel(
    copies, own, other, act_basis, basis0, basis1, basis2, basis3, eigen0, eigen1, eigen2, eigen3,
    acts, grads, columns, eigen
):
    x = lax.axis_index("x")
    for copy in copies:
        copy.wait()
    for step, part in enumerate((basis0, basis1, basis2, basis3)):
        columns[:, pl.ds(ring_slot(x, step), 128)] = part[...]
    for step, part in enumerate((eigen0, eigen1, eigen2, eigen3)):
        eigen[pl.ds(ring_slot(x, step), 128), :] = part[...].T

    def tiles(ref, first):
        return jnp.concatenate([ref[first + t] for t in range(4)], axis=1)

    def turned(rows, by):
        return rotated(rows, by).T.astype(BF)

    acts[:, 0:256] = turned(tiles(own, 0), act_basis[...])
    acts[:, 256:512] = turned(tiles(other, 0), act_basis[...])
    grads[:, 0:256] = turned(tiles(own, 8), columns[...])
    grads[:, 256:512] = turned(tiles(other, 4), columns[...])


def score_kernel(
    copies, acts, grads_in, columns, eigen, queries, act_basis, query_ids, ids, out, scale, grads
):
    c = lax.axis_index("c")
    total = 0.0
    for peer in range(8):
        total += jnp.sum(queries[peer, 256:264, :].astype(F32))
    damping = 0.1 * total / (D * FF)
    norm = float(D * FF) ** (-0.5)
    scale[...] = norm / (eigen[...] + damping)
    grads[...] = grads_in[...].astype(F32)

    def query_rows(core):
        rows = [
            jnp.concatenate([queries[4 * core + p, t * 64 : t * 64 + 64, :] for t in range(4)], axis=1)
            for p in range(4)
        ]
        return jnp.concatenate(rows, axis=0)

    for copy in copies:
        copy.wait()
    query_act = rotated(query_rows(c), act_basis[...]).astype(BF)
    query_turned = rotated(query_rows(1 - c), columns[...]).T.astype(BF)
    row = lax.broadcasted_iota(jnp.int32, (QUERIES, 512), 0)
    scores = jnp.zeros((QUERIES, 512), F32)
    for q in range(QUERIES):
        chosen = (query_ids[...] == q).astype(F32).astype(BF)
        gram = rotated(query_turned * chosen, query_act)
        precond = (gram * scale[...]).astype(BF)
        mixed = rotated(precond, acts[...])
        score = jnp.sum(mixed * grads[...], axis=0, keepdims=True)
        scores = jnp.where(row == q, score, scores)
    row = lax.broadcasted_iota(jnp.int32, (EXAMPLES, 512), 0)
    chosen = (ids[...] == row).astype(F32)
    sums = lax.dot_general(
        chosen,
        scores,
        (((1,), (1,)), ((), ())),
        precision=lax.Precision.HIGHEST,
        preferred_element_type=F32,
    )
    sums = [sums[part * 32 : part * 32 + 32, :] for part in range(4)]
    out[...] = jnp.concatenate(sums + [jnp.zeros((32, 64), F32)], axis=1)


def local_call(kernel, mib, outs, near, far, scratch=()):
    count = len(far)

    def body(*refs):
        refs = list(refs)
        held, refs = refs[: len(near)], refs[len(near) :]
        sources, refs = refs[:count], refs[count:]
        results, refs = refs[: len(outs)], refs[len(outs) :]
        buffers, refs = refs[:count], refs[count:]
        copies = []
        if count:
            done, refs = refs[0], refs[1:]
            copies = [pltpu.make_async_copy(sources[k], buffers[k], done.at[k]) for k in range(count)]
        for copy in copies:
            copy.start()
        kernel(copies, *held, *buffers, *results, *refs)

    staged = [pltpu.VMEM(array.shape, array.dtype) for array in far]
    if count:
        staged.append(pltpu.SemaphoreType.DMA((count,)))
    vmem = pl.BlockSpec(memory_space=pltpu.VMEM)
    arrays = [pltpu.with_memory_space_constraint(array, pltpu.VMEM) for array in near]
    arrays += [pltpu.with_memory_space_constraint(array, pltpu.HBM) for array in far]
    return pl.pallas_call(
        body,
        out_shape=[jax.ShapeDtypeStruct(shape, dtype) for shape, dtype in outs],
        in_specs=[vmem] * len(near) + [pl.BlockSpec(memory_space=pltpu.HBM)] * count,
        out_specs=[vmem] * len(outs),
        scratch_shapes=staged + list(scratch),
        compiler_params=pltpu.CompilerParams(vmem_limit_bytes=mib << 20),
        cost_estimate=pl.CostEstimate(flops=1000, transcendentals=0, bytes_accessed=1000),
    )(*arrays)


def ring_parts(block, way):
    def moved(part, step):
        return lax.ppermute(part, "x", [(p, (p + step) % 4) for p in range(4)])

    one, three = moved(block, 1), moved(block, 3)
    return [block, one, moved(one, 1) if way == 1 else moved(three, 3), three]


def shards(
    train_act,
    train_grad,
    query_act,
    query_grad,
    act_basis,
    grad_basis,
    eigenvalues,
    example_ids,
    query_ids,
):
    x = lax.axis_index("x")
    c = lax.axis_index("c")
    (message,) = local_call(
        pack_kernel,
        6,
        [((64, 17, 4, 128), BF)],
        (),
        (train_act, train_grad, query_act, query_grad, eigenvalues),
    )
    message, eigenvalues, grad_basis = lax.optimization_barrier((message, eigenvalues, grad_basis))
    eigens = ring_parts(eigenvalues, 3)
    bases = ring_parts(grad_basis, 1)
    got = swap_all(message, ("y", "zh", "zl"))

    ids = lax.dynamic_index_in_dim(example_ids.reshape(2, 8, 4, 4, 2, 4), x, 2, keepdims=False)
    ids = jnp.transpose(ids, (1, 0, 2, 3, 4))
    ids_own = lax.dynamic_index_in_dim(ids, c, 3, keepdims=False).reshape(1, 256)
    ids_other = lax.dynamic_index_in_dim(ids, 1 - c, 3, keepdims=False).reshape(1, 256)
    ids = jnp.concatenate([ids_own, ids_other], axis=1)
    ids = ids // 64 * 64 + ids % 2 * 32 + ids % 64 // 2
    query_order = jnp.transpose(query_ids.reshape(2, 8, 4, 4), (2, 1, 0, 3)).reshape(1, 256)
    got, eigens, bases, ids, query_order = lax.optimization_barrier((got, eigens, bases, ids, query_order))

    (queries,) = local_call(relay_kernel, 6, [((8, 264, 128), BF)], (got,), ())
    queries, got = lax.optimization_barrier((queries, got))
    queries = swap_all(queries, ("c", "x"))
    other = lax.ppermute(got, "c", [(0, 1), (1, 0)])
    own = jnp.transpose(got[:, 0:12], (1, 0, 2, 3)).reshape(12, 256, 128)
    other = jnp.transpose(other[:, 4:12], (1, 0, 2, 3)).reshape(8, 256, 128)
    held = local_call(
        turn_kernel,
        12,
        [((512, 512), BF), ((512, 512), BF), ((512, 512), BF), ((512, 512), F32)],
        (own, other),
        (act_basis, *bases, *eigens),
    )
    (partial_scores,) = local_call(
        score_kernel,
        20,
        [((32, 128), F32)],
        (*held, queries),
        (act_basis, query_order, ids),
        (pltpu.VMEM((512, 512), F32), pltpu.VMEM((512, 512), F32)),
    )
    sums = jnp.sum(swap_all(partial_scores, ("y", "x")), axis=0, keepdims=True)
    sums = jnp.sum(swap_all(jnp.broadcast_to(sums, (16, 128)), ("zh", "zl", "c")), axis=0)
    return lax.dynamic_slice_in_dim(sums, lax.axis_index("zh") * 32, 32, 0).reshape(2, 16)


def solution(mesh):
    fine = Mesh(np.asarray(mesh.devices).reshape(SIZES), DP + BLK)
    placed = (
        P(DP + BLK, None),
        P(DP + BLK, None),
        P(DP, BLK),
        P(DP, None),
        P(BLK, None),
        P(None, DP),
        P(BLK, DP),
        P(),
        P(),
    )
    return jax.shard_map(
        shards, mesh=fine, in_specs=placed, out_specs=P(DP, None), check_vma=False
    )
```

```python
import jax
import jax.numpy as jnp
import numpy as np
from jax import lax
from jax.experimental import pallas as pl
from jax.experimental.pallas import tpu as pltpu
from jax.sharding import Mesh, PartitionSpec as P

D = 4096
FF = 8192
QUERIES = 16
EXAMPLES = 128
BF = jnp.bfloat16
F32 = jnp.float32
DP = ("zh", "y", "x")
BLK = ("zl", "c")
SIZES = (2, 8, 4, 4, 2)


def swap_all(block, axes):
    return lax.all_to_all(block, axes, split_axis=0, concat_axis=0, tiled=True)


def three_parts(rows):
    high = rows.astype(BF).astype(F32)
    rest = rows - high
    mid = rest.astype(BF).astype(F32)
    return high, mid, rest - mid


def pack_kernel(copies, act, grad, query_act, query_grad, eigen, out):
    zl, c = lax.axis_index("zl"), lax.axis_index("c")
    for copy in copies:
        copy.wait()
    sums = jnp.sum(jnp.sum(eigen[...].reshape(64, 8, 128), axis=0), axis=0, keepdims=True)
    sums = jnp.concatenate([*three_parts(sums), jnp.zeros((1, 128), F32)], axis=0).astype(BF)
    for z in range(4):
        own = act[:, pl.ds(pl.multiple_of(z * 1024 + c * 512, 128), 512)]
        away = act[:, pl.ds(pl.multiple_of(z * 1024 + 512 - c * 512, 128), 512)]
        for k in range(16):
            to, m = k * 4 + z, k % 2 * 8 + k // 2
            for t in range(4):
                part = slice(t * 128, t * 128 + 128)
                cols = slice(m * 512 + t * 128, m * 512 + t * 128 + 128)
                out[to, t] = own[:, part]
                out[to, 4 + t] = away[:, part]
                out[to, 8 + t] = grad[:, cols]
                out[to, 12 + t] = query_grad[:, cols]
            out[to, 16] = sums
    for m in range(16):
        for t in range(4):
            out[m * 4 + zl, 12 + t] = query_act[:, t * 128 : t * 128 + 128]


def relay_kernel(copies, got, out):
    zl, c = lax.axis_index("zl"), lax.axis_index("c")
    sums = jnp.sum(jnp.sum(got[:, 16].astype(F32), axis=0), axis=0, keepdims=True)
    sums = jnp.concatenate([*three_parts(sums), jnp.zeros((5, 128), F32)], axis=0).astype(BF)
    for core in range(2):
        source = zl + jnp.where(c == core, 0, 1 - 2 * (zl % 2))
        for t in range(4):
            for s in range(16):
                out[4 * core, t * 64 + s * 4 : t * 64 + s * 4 + 4, :] = got[s * 4 + source, 12 + t]
        out[4 * core, 256:264, :] = sums
        for x in range(1, 4):
            out[4 * core + x] = out[4 * core]


def rotated(rows, by):
    return jnp.dot(rows, by, preferred_element_type=F32)


def ring_slot(x, step):
    return pl.multiple_of(lax.rem(x + 4 - step, 4) * 128, 128)


def turn_kernel(
    copies, own, other, act_basis, basis0, basis1, basis2, basis3, eigen0, eigen1, eigen2, eigen3,
    acts, grads, columns, eigen
):
    x = lax.axis_index("x")
    for copy in copies:
        copy.wait()
    for step, part in enumerate((basis0, basis1, basis2, basis3)):
        columns[:, pl.ds(ring_slot(x, step), 128)] = part[...]
    for step, part in enumerate((eigen0, eigen1, eigen2, eigen3)):
        eigen[pl.ds(ring_slot(x, step), 128), :] = part[...].T

    def tiles(ref, first):
        return jnp.concatenate([ref[first + t] for t in range(4)], axis=1)

    def turned(rows, by):
        return rotated(rows, by).T.astype(BF)

    acts[:, 0:256] = turned(tiles(own, 0), act_basis[...])
    acts[:, 256:512] = turned(tiles(other, 0), act_basis[...])
    grads[:, 0:256] = turned(tiles(own, 8), columns[...])
    grads[:, 256:512] = turned(tiles(other, 4), columns[...])


def score_kernel(
    copies, acts, grads_in, columns, eigen, queries, act_basis, query_ids, ids, out, scale, grads
):
    c = lax.axis_index("c")
    total = 0.0
    for peer in range(8):
        total += jnp.sum(queries[peer, 256:264, :].astype(F32))
    damping = 0.1 * total / (D * FF)
    norm = float(D * FF) ** (-0.5)
    scale[...] = norm / (eigen[...] + damping)
    grads[...] = grads_in[...].astype(F32)

    def query_rows(core):
        rows = [
            jnp.concatenate([queries[4 * core + p, t * 64 : t * 64 + 64, :] for t in range(4)], axis=1)
            for p in range(4)
        ]
        return jnp.concatenate(rows, axis=0)

    for copy in copies:
        copy.wait()
    query_act = rotated(query_rows(c), act_basis[...]).astype(BF)
    query_turned = rotated(query_rows(1 - c), columns[...]).T.astype(BF)
    row = lax.broadcasted_iota(jnp.int32, (QUERIES, 512), 0)
    scores = jnp.zeros((QUERIES, 512), F32)
    for q in range(QUERIES):
        chosen = (query_ids[...] == q).astype(F32).astype(BF)
        gram = rotated(query_turned * chosen, query_act)
        precond = (gram * scale[...]).astype(BF)
        mixed = rotated(precond, acts[...])
        score = jnp.sum(mixed * grads[...], axis=0, keepdims=True)
        scores = jnp.where(row == q, score, scores)
    row = lax.broadcasted_iota(jnp.int32, (EXAMPLES, 512), 0)
    chosen = (ids[...] == row).astype(F32)
    sums = lax.dot_general(
        chosen,
        scores,
        (((1,), (1,)), ((), ())),
        precision=lax.Precision.HIGHEST,
        preferred_element_type=F32,
    )
    out[...] = jnp.concatenate([sums[part * 8 : part * 8 + 8, :] for part in range(16)], axis=1)


def local_call(kernel, mib, outs, near, far, scratch=()):
    count = len(far)

    def body(*refs):
        refs = list(refs)
        held, refs = refs[: len(near)], refs[len(near) :]
        sources, refs = refs[:count], refs[count:]
        results, refs = refs[: len(outs)], refs[len(outs) :]
        buffers, refs = refs[:count], refs[count:]
        copies = []
        if count:
            done, refs = refs[0], refs[1:]
            copies = [pltpu.make_async_copy(sources[k], buffers[k], done.at[k]) for k in range(count)]
        for copy in copies:
            copy.start()
        kernel(copies, *held, *buffers, *results, *refs)

    staged = [pltpu.VMEM(array.shape, array.dtype) for array in far]
    if count:
        staged.append(pltpu.SemaphoreType.DMA((count,)))
    vmem = pl.BlockSpec(memory_space=pltpu.VMEM)
    arrays = [pltpu.with_memory_space_constraint(array, pltpu.VMEM) for array in near]
    arrays += [pltpu.with_memory_space_constraint(array, pltpu.HBM) for array in far]
    return pl.pallas_call(
        body,
        out_shape=[jax.ShapeDtypeStruct(shape, dtype) for shape, dtype in outs],
        in_specs=[vmem] * len(near) + [pl.BlockSpec(memory_space=pltpu.HBM)] * count,
        out_specs=[vmem] * len(outs),
        scratch_shapes=staged + list(scratch),
        compiler_params=pltpu.CompilerParams(vmem_limit_bytes=mib << 20),
        cost_estimate=pl.CostEstimate(flops=1000, transcendentals=0, bytes_accessed=1000),
    )(*arrays)


def ring_parts(block, way):
    def moved(part, step):
        return lax.ppermute(part, "x", [(p, (p + step) % 4) for p in range(4)])

    one, three = moved(block, 1), moved(block, 3)
    return [block, one, moved(one, 1) if way == 1 else moved(three, 3), three]


def shards(
    train_act,
    train_grad,
    query_act,
    query_grad,
    act_basis,
    grad_basis,
    eigenvalues,
    example_ids,
    query_ids,
):
    x = lax.axis_index("x")
    c = lax.axis_index("c")
    (message,) = local_call(
        pack_kernel,
        6,
        [((64, 17, 4, 128), BF)],
        (),
        (train_act, train_grad, query_act, query_grad, eigenvalues),
    )
    message, eigenvalues, grad_basis = lax.optimization_barrier((message, eigenvalues, grad_basis))
    eigens = ring_parts(eigenvalues, 3)
    bases = ring_parts(grad_basis, 1)
    got = swap_all(message, ("y", "zh", "zl"))

    ids = lax.dynamic_index_in_dim(example_ids.reshape(2, 8, 4, 4, 2, 4), x, 2, keepdims=False)
    ids = jnp.transpose(ids, (1, 0, 2, 3, 4))
    ids_own = lax.dynamic_index_in_dim(ids, c, 3, keepdims=False).reshape(1, 256)
    ids_other = lax.dynamic_index_in_dim(ids, 1 - c, 3, keepdims=False).reshape(1, 256)
    ids = jnp.concatenate([ids_own, ids_other], axis=1)
    ids = ids // 64 * 64 + ids % 8 * 8 + ids % 64 // 8
    query_order = jnp.transpose(query_ids.reshape(2, 8, 4, 4), (2, 1, 0, 3)).reshape(1, 256)
    got, eigens, bases, ids, query_order = lax.optimization_barrier((got, eigens, bases, ids, query_order))

    (queries,) = local_call(relay_kernel, 6, [((8, 264, 128), BF)], (got,), ())
    queries, got = lax.optimization_barrier((queries, got))
    queries = swap_all(queries, ("c", "x"))
    other = lax.ppermute(got, "c", [(0, 1), (1, 0)])
    own = jnp.transpose(got[:, 0:12], (1, 0, 2, 3)).reshape(12, 256, 128)
    other = jnp.transpose(other[:, 4:12], (1, 0, 2, 3)).reshape(8, 256, 128)
    held = local_call(
        turn_kernel,
        12,
        [((512, 512), BF), ((512, 512), BF), ((512, 512), BF), ((512, 512), F32)],
        (own, other),
        (act_basis, *bases, *eigens),
    )
    (partial_scores,) = local_call(
        score_kernel,
        20,
        [((8, 256), F32)],
        (*held, queries),
        (act_basis, query_order, ids),
        (pltpu.VMEM((512, 512), F32), pltpu.VMEM((512, 512), F32)),
    )
    partial_scores = jnp.concatenate([partial_scores, partial_scores], axis=0)
    sums = jnp.sum(swap_all(partial_scores, ("c", "y")), axis=0, keepdims=True)
    sums = jnp.sum(swap_all(jnp.broadcast_to(sums, (32, 256)), ("zh", "zl", "x")), axis=0)
    place = lax.axis_index("zh") * 128 + x * 32
    return lax.dynamic_slice_in_dim(sums, place, 32, 0).reshape(2, 16)


def solution(mesh):
    fine = Mesh(np.asarray(mesh.devices).reshape(SIZES), DP + BLK)
    placed = (
        P(DP + BLK, None),
        P(DP + BLK, None),
        P(DP, BLK),
        P(DP, None),
        P(BLK, None),
        P(None, DP),
        P(BLK, DP),
        P(),
        P(),
    )
    return jax.shard_map(
        shards, mesh=fine, in_specs=placed, out_specs=P(DP, None), check_vma=False
    )
```

```python
import jax
import jax.numpy as jnp
import numpy as np
from jax import lax
from jax.experimental import pallas as pl
from jax.experimental.pallas import tpu as pltpu
from jax.sharding import Mesh, PartitionSpec as P

D = 4096
FF = 8192
QUERIES = 16
EXAMPLES = 128
BF = jnp.bfloat16
F32 = jnp.float32
DP = ("zh", "y", "x")
BLK = ("zl", "c")
SIZES = (2, 8, 4, 4, 2)


def swap_all(block, axes):
    return lax.all_to_all(block, axes, split_axis=0, concat_axis=0, tiled=True)


def three_parts(rows):
    high = rows.astype(BF).astype(F32)
    rest = rows - high
    mid = rest.astype(BF).astype(F32)
    return high, mid, rest - mid


def pack_kernel(copies, act, grad, query_act, query_grad, eigen, out):
    zl, c = lax.axis_index("zl"), lax.axis_index("c")
    for copy in copies:
        copy.wait()
    sums = jnp.sum(jnp.sum(eigen[...].reshape(64, 8, 128), axis=0), axis=0, keepdims=True)
    sums = jnp.concatenate([*three_parts(sums), jnp.zeros((1, 128), F32)], axis=0).astype(BF)
    for z in range(4):
        own = act[:, pl.ds(pl.multiple_of(z * 1024 + c * 512, 128), 512)]
        away = act[:, pl.ds(pl.multiple_of(z * 1024 + 512 - c * 512, 128), 512)]
        for k in range(16):
            to, m = k * 4 + z, k
            for t in range(4):
                part = slice(t * 128, t * 128 + 128)
                cols = slice(m * 512 + t * 128, m * 512 + t * 128 + 128)
                out[to, t] = own[:, part]
                out[to, 4 + t] = away[:, part]
                out[to, 8 + t] = grad[:, cols]
                out[to, 12 + t] = query_grad[:, cols]
            out[to, 16] = sums
    for m in range(16):
        for t in range(4):
            out[m * 4 + zl, 12 + t] = query_act[:, t * 128 : t * 128 + 128]


def relay_kernel(copies, got, out):
    zl, c = lax.axis_index("zl"), lax.axis_index("c")
    sums = jnp.sum(jnp.sum(got[:, 16].astype(F32), axis=0), axis=0, keepdims=True)
    sums = jnp.concatenate([*three_parts(sums), jnp.zeros((5, 128), F32)], axis=0).astype(BF)
    for core in range(2):
        source = zl + jnp.where(c == core, 0, 1 - 2 * (zl % 2))
        for t in range(4):
            for s in range(16):
                out[4 * core, t * 64 + s * 4 : t * 64 + s * 4 + 4, :] = got[s * 4 + source, 12 + t]
        out[4 * core, 256:264, :] = sums
        for x in range(1, 4):
            out[4 * core + x] = out[4 * core]


def rotated(rows, by):
    return jnp.dot(rows, by, preferred_element_type=F32)


def ring_slot(x, step):
    return pl.multiple_of(lax.rem(x + 4 - step, 4) * 128, 128)


def turn_kernel(
    copies, own, other, act_basis, basis0, basis1, basis2, basis3, eigen0, eigen1, eigen2, eigen3,
    acts, grads, columns, eigen
):
    x = lax.axis_index("x")
    for copy in copies:
        copy.wait()
    for step, part in enumerate((basis0, basis1, basis2, basis3)):
        columns[:, pl.ds(ring_slot(x, step), 128)] = part[...]
    for step, part in enumerate((eigen0, eigen1, eigen2, eigen3)):
        eigen[pl.ds(ring_slot(x, step), 128), :] = part[...].T

    def tiles(ref, first):
        return jnp.concatenate([ref[first + t] for t in range(4)], axis=1)

    def turned(rows, by):
        return rotated(rows, by).T.astype(BF)

    acts[:, 0:256] = turned(tiles(own, 0), act_basis[...])
    acts[:, 256:512] = turned(tiles(other, 0), act_basis[...])
    grads[:, 0:256] = turned(tiles(own, 8), columns[...])
    grads[:, 256:512] = turned(tiles(other, 4), columns[...])


def score_kernel(
    copies, acts, grads_in, columns, eigen, queries, act_basis, query_ids, ids, out, scale, grads
):
    c = lax.axis_index("c")
    total = 0.0
    for peer in range(8):
        total += jnp.sum(queries[peer, 256:264, :].astype(F32))
    damping = 0.1 * total / (D * FF)
    norm = float(D * FF) ** (-0.5)
    scale[...] = norm / (eigen[...] + damping)
    grads[...] = grads_in[...].astype(F32)

    def query_rows(core):
        rows = [
            jnp.concatenate([queries[4 * core + p, t * 64 : t * 64 + 64, :] for t in range(4)], axis=1)
            for p in range(4)
        ]
        return jnp.concatenate(rows, axis=0)

    for copy in copies:
        copy.wait()
    query_act = rotated(query_rows(c), act_basis[...]).astype(BF)
    query_turned = rotated(query_rows(1 - c), columns[...]).T.astype(BF)
    row = lax.broadcasted_iota(jnp.int32, (QUERIES, 512), 0)
    scores = jnp.zeros((QUERIES, 512), F32)
    for q in range(QUERIES):
        chosen = (query_ids[...] == q).astype(F32).astype(BF)
        gram = rotated(query_turned * chosen, query_act)
        precond = (gram * scale[...]).astype(BF)
        mixed = rotated(precond, acts[...])
        score = jnp.sum(mixed * grads[...], axis=0, keepdims=True)
        scores = jnp.where(row == q, score, scores)
    row = lax.broadcasted_iota(jnp.int32, (EXAMPLES, 512), 0)
    chosen = (ids[...] == row).astype(F32)
    sums = lax.dot_general(
        chosen,
        scores,
        (((1,), (1,)), ((), ())),
        precision=lax.Precision.HIGHEST,
        preferred_element_type=F32,
    )
    out[...] = jnp.concatenate([sums[part * 8 : part * 8 + 8, :] for part in range(16)], axis=1)


def local_call(kernel, mib, outs, near, far, scratch=()):
    count = len(far)

    def body(*refs):
        refs = list(refs)
        held, refs = refs[: len(near)], refs[len(near) :]
        sources, refs = refs[:count], refs[count:]
        results, refs = refs[: len(outs)], refs[len(outs) :]
        buffers, refs = refs[:count], refs[count:]
        copies = []
        if count:
            done, refs = refs[0], refs[1:]
            copies = [pltpu.make_async_copy(sources[k], buffers[k], done.at[k]) for k in range(count)]
        for copy in copies:
            copy.start()
        kernel(copies, *held, *buffers, *results, *refs)

    staged = [pltpu.VMEM(array.shape, array.dtype) for array in far]
    if count:
        staged.append(pltpu.SemaphoreType.DMA((count,)))
    vmem = pl.BlockSpec(memory_space=pltpu.VMEM)
    arrays = [pltpu.with_memory_space_constraint(array, pltpu.VMEM) for array in near]
    arrays += [pltpu.with_memory_space_constraint(array, pltpu.HBM) for array in far]
    return pl.pallas_call(
        body,
        out_shape=[jax.ShapeDtypeStruct(shape, dtype) for shape, dtype in outs],
        in_specs=[vmem] * len(near) + [pl.BlockSpec(memory_space=pltpu.HBM)] * count,
        out_specs=[vmem] * len(outs),
        scratch_shapes=staged + list(scratch),
        compiler_params=pltpu.CompilerParams(vmem_limit_bytes=mib << 20),
        cost_estimate=pl.CostEstimate(flops=1000, transcendentals=0, bytes_accessed=1000),
    )(*arrays)


def ring_parts(block, way):
    def moved(part, step):
        return lax.ppermute(part, "x", [(p, (p + step) % 4) for p in range(4)])

    one, three = moved(block, 1), moved(block, 3)
    return [block, one, moved(one, 1) if way == 1 else moved(three, 3), three]


def shards(
    train_act,
    train_grad,
    query_act,
    query_grad,
    act_basis,
    grad_basis,
    eigenvalues,
    example_ids,
    query_ids,
):
    x = lax.axis_index("x")
    c = lax.axis_index("c")
    (message,) = local_call(
        pack_kernel,
        6,
        [((64, 17, 4, 128), BF)],
        (),
        (train_act, train_grad, query_act, query_grad, eigenvalues),
    )
    message, eigenvalues, grad_basis = lax.optimization_barrier((message, eigenvalues, grad_basis))
    eigens = ring_parts(eigenvalues, 3)
    bases = ring_parts(grad_basis, 1)
    got = swap_all(message, ("zh", "y", "zl"))

    ids = lax.dynamic_index_in_dim(example_ids.reshape(2, 8, 4, 4, 2, 4), x, 2, keepdims=False)
    ids_own = lax.dynamic_index_in_dim(ids, c, 3, keepdims=False).reshape(1, 256)
    ids_other = lax.dynamic_index_in_dim(ids, 1 - c, 3, keepdims=False).reshape(1, 256)
    ids = jnp.concatenate([ids_own, ids_other], axis=1)
    ids = ids // 64 * 64 + ids % 8 * 8 + ids % 64 // 8
    query_order = jnp.transpose(query_ids.reshape(2, 8, 4, 4), (2, 0, 1, 3)).reshape(1, 256)
    got, eigens, bases, ids, query_order = lax.optimization_barrier((got, eigens, bases, ids, query_order))

    (queries,) = local_call(relay_kernel, 6, [((8, 264, 128), BF)], (got,), ())
    queries, got = lax.optimization_barrier((queries, got))
    queries = swap_all(queries, ("c", "x"))
    other = lax.ppermute(got, "c", [(0, 1), (1, 0)])
    own = jnp.transpose(got[:, 0:12], (1, 0, 2, 3)).reshape(12, 256, 128)
    other = jnp.transpose(other[:, 4:12], (1, 0, 2, 3)).reshape(8, 256, 128)
    held = local_call(
        turn_kernel,
        12,
        [((512, 512), BF), ((512, 512), BF), ((512, 512), BF), ((512, 512), F32)],
        (own, other),
        (act_basis, *bases, *eigens),
    )
    (partial_scores,) = local_call(
        score_kernel,
        20,
        [((8, 256), F32)],
        (*held, queries),
        (act_basis, query_order, ids),
        (pltpu.VMEM((512, 512), F32), pltpu.VMEM((512, 512), F32)),
    )
    partial_scores = jnp.concatenate([partial_scores, partial_scores], axis=0)
    sums = jnp.sum(swap_all(partial_scores, ("c", "y")), axis=0, keepdims=True)
    sums = jnp.sum(swap_all(jnp.broadcast_to(sums, (32, 256)), ("zh", "zl", "x")), axis=0)
    place = lax.axis_index("zh") * 128 + x * 32
    return lax.dynamic_slice_in_dim(sums, place, 32, 0).reshape(2, 16)


def solution(mesh):
    fine = Mesh(np.asarray(mesh.devices).reshape(SIZES), DP + BLK)
    placed = (
        P(DP + BLK, None),
        P(DP + BLK, None),
        P(DP, BLK),
        P(DP, None),
        P(BLK, None),
        P(None, DP),
        P(BLK, DP),
        P(),
        P(),
    )
    return jax.shard_map(
        shards, mesh=fine, in_specs=placed, out_specs=P(DP, None), check_vma=False
    )
```
